128 devices in a mesh: vars: 64 (over x, y, z), samp: 2 (over core).
Axes of the slice: x: 4, y: 4, z: 4, core: 2. Of those that a mesh axis runs over, the one named last changes fastest.
Arguments:
- voxel_data: bfloat16 [131072, 1536], P('vars', 'samp'), may hold values from -6 to 6
- omega_blocks: float32 [1024, 8, 128, 128], P('vars'), may hold values from -0.3 to 3, as said below
- block_cols: int32 [1024, 8], P('vars'), may hold values from 0 to 1023, as said below
Outputs:
- gradient: float32 [1024, 8, 128, 128], P('vars', None, 'samp')
- omega_next: float32 [1024, 8, 128, 128], P('vars', None, 'samp')
The draws below stay inside these ranges and needn't reach their ends.
Inputs may be any that keep to these rules, and one draw needn't show every extreme that they name: Block row i is held with the rows of its device. block_cols[i, 0] = i. For s >= 1, block_cols[i, s] = j is a block row of another device, and block_cols[j, s] = i. A row names no block twice. The rows of one device name at most 2 blocks of any one other device, and exactly that many for some pair. The diagonal entries of omega_blocks[i, 0] lie between 1 and 3; all other entries lie between -0.3 and 0.3.
All inputs are finite; a program needn't handle non-finite values.
Results may differ from the reference program's by a relative error of at most 0.0034.
Values may be sent and summed in bfloat16 or wider, within the bound.
A program may use at most 192 MiB of HBM per device.

```python
import jax
import jax.numpy as jnp
from jax import lax

BLOCK = 128
SLOTS = 8
ROWS_DEV = 16
BLOCK_ROWS = 1024
VOXELS = 131072
SAMPLES = 1536
N_VARS = 64


def draw_block_cols(key, part):
    keys = jax.random.split(jax.random.fold_in(key, 11), 4)
    peer_count = N_VARS - 1
    shuffled = jax.random.permutation(keys[0], peer_count)
    offset = jax.random.randint(keys[1], (), 0, peer_count)
    target = N_VARS // 2 - 1
    where_target = jnp.argmax((shuffled == target).astype(jnp.int32))
    order = shuffled.at[where_target].set(shuffled[offset]).at[offset].set(target)
    flips = jax.random.randint(keys[2], (SLOTS,), 0, 2)
    relabel = jax.random.permutation(keys[3], ROWS_DEV)
    undo = jnp.argsort(relabel)
    row_ids = jnp.arange(BLOCK_ROWS)
    device = row_ids // ROWS_DEV
    labels = relabel[row_ids % ROWS_DEV]
    groups = labels // 2
    positions = jnp.arange(1, SLOTS)
    serial = groups[:, None] * (SLOTS - 1) + (positions[None, :] - 1)
    masks = order[(serial + offset) % peer_count] + 1
    partner_dev = jnp.bitwise_xor(device[:, None], masks)
    partner_label = jnp.bitwise_xor(labels[:, None], flips[1:][None, :])
    columns = partner_dev * ROWS_DEV + undo[partner_label]
    return jnp.concatenate([row_ids[:, None], columns], axis=1).astype(jnp.int32)


def draw_omega_blocks(key, part):
    first, second = jax.random.split(jax.random.fold_in(key, 23))
    shape = (BLOCK_ROWS, SLOTS, BLOCK, BLOCK)
    spread = 0.05 * jax.random.truncated_normal(first, -6.0, 6.0, shape, jnp.float32)
    diagonal = jax.random.uniform(second, (BLOCK_ROWS, BLOCK), jnp.float32, 1.0, 3.0)
    identity = jnp.eye(BLOCK, dtype=jnp.float32)
    first_slot = (jnp.arange(SLOTS) == 0).astype(jnp.float32)[None, :, None, None]
    placed = first_slot * identity[None, None] * diagonal[:, None, :, None]
    return spread * (1.0 - first_slot * identity[None, None]) + placed


def steps_of(key, dims, shards, low, largest):
    def one(axis_at, parts):
        heights = jax.random.uniform(jax.random.fold_in(jax.random.fold_in(key, 6), axis_at), (parts,), jnp.float32, low / len(shards), largest / len(shards))
        return jnp.repeat(jnp.exp(heights), dims[axis_at] // parts).reshape((-1,) + (1,) * (len(dims) - axis_at - 1))

    factor_of = one(*shards[0])
    for cut in shards[1:]:
        factor_of = factor_of * one(*cut)
    return factor_of


def bell_draw(rng, shape, deviation, limit, pieces=(), held_as=jnp.bfloat16):
    entries = jax.random.normal(rng, shape, jnp.float32) * deviation
    if len(pieces) > 0:
        entries = steps_of(rng, shape, pieces, -0.22, 0.18) * entries
    return jnp.clip(entries, min=-limit, max=limit).astype(held_as)


def setup_inputs(seed: int = 0) -> dict:
    streams_of = jax.random.split(jax.random.key(seed), 4)
    return {
        "voxel_data": bell_draw(streams_of[0], (VOXELS, SAMPLES), 1.0, 6.0, ((0, 64), (1, 2))),
        "omega_blocks": draw_omega_blocks(jax.random.fold_in(streams_of[3], 71), 0),
        "block_cols": draw_block_cols(jax.random.fold_in(streams_of[3], 71), 0),
    }


STEP = 0.5
PENALTY = 0.1


def reference(voxel_data, omega_blocks, block_cols):
    block_width = omega_blocks.shape[2]
    sample_total = voxel_data.shape[1]
    panels = voxel_data.reshape(BLOCK_ROWS, block_width, sample_total)
    omega_low = omega_blocks.astype(jnp.bfloat16)

    def row_product(pair):
        blocks, columns = pair
        chosen = jnp.take(panels, columns, axis=0).astype(jnp.float32)
        summed = jnp.einsum('kab,kbn->an', blocks.astype(jnp.float32), chosen)
        rounded = lax.optimization_barrier(summed.astype(jnp.bfloat16))
        w_row = rounded.astype(jnp.float32)
        return jnp.einsum('an,kbn->kab', w_row, chosen)

    grams = lax.map(row_product, (omega_low, block_cols))
    mirror = grams[block_cols, jnp.arange(SLOTS, dtype=jnp.int32)[None, :]]
    gradient = (grams + jnp.swapaxes(mirror, 2, 3)) * (0.5 / sample_total)
    diagonal = jnp.diagonal(omega_blocks[:, 0], axis1=1, axis2=2)
    identity = jnp.eye(block_width, dtype=jnp.float32)
    gradient = gradient.at[:, 0].add(-identity[None] * (1.0 / diagonal)[:, :, None])
    trial = omega_blocks - STEP * gradient
    shrunk = jnp.sign(trial) * jnp.maximum(jnp.abs(trial) - STEP * PENALTY, 0.0)
    first_slot = (jnp.arange(SLOTS) == 0)[None, :, None, None]
    on_diagonal = jnp.logical_and(first_slot, identity[None, None] > 0.5)
    omega_next = jnp.where(on_diagonal, trial, shrunk)
    return gradient, omega_next
```

```python
import functools

import jax
import jax.numpy as jnp
from jax import lax
from jax.experimental import pallas as pl
from jax.experimental.pallas import tpu as pltpu
from jax.sharding import PartitionSpec as P

STEP = 0.5
PENALTY = 0.1
MESH = pl.DeviceIdType.MESH
RING = 4
STRIDES = (16, 4, 1)
BW = 128
ROWS = 16
SLOTS = 8
ENTRIES = ROWS * SLOTS
LANES = 128
PARTS = 6
NEAR = (1, 3, 2)
CUTS = (((0, 16), (0, 16)), ((16, 32), (16, 48)), ((32, 64), (48, 64)))


def place():
    v = lax.axis_index("vars")
    at = (v // 16, lax.rem(v // 4, RING), lax.rem(v, RING))
    return v, at, lax.axis_index("samp")


def orders(r):
    return r % 3, (r + 1) % 3, (r + 2) % 3


def moved(v, at, axis, delta):
    there = lax.rem(at[axis] + delta, RING)
    return there, v + (there - at[axis]) * STRIDES[axis]


def meet(v, at, h, sibling):
    barrier = pltpu.get_barrier_semaphore()
    for axis in range(3):
        for delta in NEAR:
            pl.semaphore_signal(
                barrier, inc=1, device_id=(moved(v, at, axis, delta)[1], h), device_id_type=MESH
            )
    if sibling:
        pl.semaphore_signal(barrier, inc=1, device_id=(v, 1 - h), device_id_type=MESH)
    pl.semaphore_wait(barrier, 10 if sibling else 9)


class Ring:
    def __init__(self, v, at, h, axis, source, landing, send, recv):
        self.v, self.at, self.h, self.axis = v, at, h, axis
        self.source, self.landing, self.send, self.recv = source, landing, send, recv

    def remote(self, delta):
        there, target = moved(self.v, self.at, self.axis, delta)
        mine = self.at[self.axis]
        return pltpu.make_async_remote_copy(
            src_ref=self.source(there, delta),
            dst_ref=self.landing(mine),
            send_sem=self.send(delta),
            recv_sem=self.recv(mine),
            device_id=(target, self.h),
            device_id_type=MESH,
        )

    def arriving(self, delta):
        there, target = moved(self.v, self.at, self.axis, delta)
        return pltpu.make_async_remote_copy(
            src_ref=self.source(there, delta),
            dst_ref=self.landing(there),
            send_sem=self.send(delta),
            recv_sem=self.recv(there),
            device_id=(target, self.h),
            device_id_type=MESH,
        )

    def local(self):
        mine = self.at[self.axis]
        return pltpu.make_async_copy(self.source(mine, 0), self.landing(mine), self.recv(mine))

    def start(self):
        for delta in NEAR:
            self.remote(delta).start()
        self.local().start()

    def wait_recv(self):
        for delta in NEAR:
            self.arriving(delta).wait_recv()
        self.local().wait()

    def wait_send(self):
        for delta in NEAR:
            self.remote(delta).wait_send()


def panel_kernel(
    x_ref, om_ref, tab_ref, idx_ref,
    own_ref, sib_ref, s2_ref,
    ag0, ag1, ag2, ag3, ag4, ag5,
    fin0, fin1, fin2, fin3, fin4, fin5,
    st, sto, gt, xc, omv, rt, tabv, tabs,
    tab_s, tab_r, tab_c, s1s, s1r, s2s, s2r, s3s, s3r, om_sem, own_sem, sib_s, sib_r,
):
    v, at, h = place()
    ag = (ag0, ag1, ag2, ag3, ag4, ag5)
    fin = (fin0, fin1, fin2, fin3, fin4, fin5)
    meet(v, at, h, True)

    tables = [
        Ring(
            v, at, h, axis,
            lambda there, delta: tab_ref,
            lambda mine, axis=axis: tabv.at[axis, mine],
            lambda delta, axis=axis: tab_s.at[axis, delta],
            lambda mine, axis=axis: tab_r.at[axis, mine],
        )
        for axis in range(3)
    ]

    def first(p):
        return Ring(
            v, at, h, orders(p)[0],
            lambda there, delta: x_ref.at[:, :, pl.ds(p * LANES, LANES)],
            lambda mine: ag[p].at[pl.ds(mine * ROWS, ROWS)],
            lambda delta: s1s.at[p, delta],
            lambda mine: s1r.at[p, mine],
        )

    def second(p):
        return Ring(
            v, at, h, orders(p)[1],
            lambda there, delta: st.at[p % 3, delta - 1] if delta else sto,
            lambda mine: s2_ref.at[p, :, pl.ds(mine * 8, 8)],
            lambda delta: s2s.at[p, delta],
            lambda mine: s2r.at[p, mine],
        )

    def third(p):
        return Ring(
            v, at, h, orders(p)[2],
            lambda there, delta: s2_ref.at[p, there],
            lambda mine: fin[p].at[pl.ds(mine * 32, 32)],
            lambda delta: s3s.at[p, delta],
            lambda mine: s3r.at[p, mine],
        )

    def stage(p):
        a_axis, b_axis, c_axis = orders(p)
        ring = second(p)
        for delta in (1, 3, 2, 0):
            there = lax.rem(at[b_axis] + delta, RING)
            base = at[a_axis] * STRIDES[a_axis] + there * STRIDES[b_axis]
            held = st.at[p % 3, delta - 1] if delta else sto

            def fill(c, carry):
                target = base + c * STRIDES[c_axis]
                for m in range(8):
                    entry = tabs[a_axis, m // 2, m % 2, target]
                    held[c, m] = ag[p][(m // 2) * ROWS + lax.div(entry, SLOTS)]
                return carry

            lax.fori_loop(0, RING, fill, 0)
            if delta:
                ring.remote(delta).start()
            else:
                ring.local().start()

    def omega(i, slot):
        return pltpu.make_async_copy(om_ref.at[i], omv.at[slot], om_sem.at[slot])

    def to_sibling(i):
        return pltpu.make_async_remote_copy(
            src_ref=st.at[i // 12, lax.rem(i // 4, 3), lax.rem(i, 4)],
            dst_ref=sib_ref.at[i],
            send_sem=sib_s.at[i],
            recv_sem=sib_r.at[i],
            device_id=(v, 1 - h),
            device_id_type=MESH,
        )

    def keep(i):
        return pltpu.make_async_copy(gt.at[i], own_ref.at[i], own_sem.at[i])

    mine_rows = pl.multiple_of(h * 64, 64)
    their_rows = pl.multiple_of((1 - h) * 64, 64)

    def compute(group):
        omega(0, 0).start()

        def row(i, carry):
            slot = lax.rem(i, 2)
            omega(i, slot).wait()

            @pl.when(i + 1 < ROWS)
            def _():
                omega(i + 1, 1 - slot).start()

            for q in range(3):
                p = group * 3 + q
                cols = pl.ds(q * LANES, LANES)
                xc[0:BW, cols] = ag[p][at[orders(p)[0]] * ROWS + i]
                for s in range(1, SLOTS):
                    xc[s * BW : (s + 1) * BW, cols] = fin[p][idx_ref[q, i * SLOTS + s]]
            blocks = omv[slot].astype(jnp.bfloat16)
            lhs = jnp.concatenate([blocks[s] for s in range(SLOTS)], axis=1)
            w = jnp.dot(lhs, xc[...], preferred_element_type=jnp.float32).astype(jnp.bfloat16)
            turned = lax.dot_general(
                xc[...], w, (((1,), (1,)), ((), ())), preferred_element_type=jnp.float32
            ).reshape(SLOTS, BW, BW)
            if group == 0:
                gt[i] = turned
            else:
                total = gt[i] + turned
                gt[i] = total
                for s in range(SLOTS):
                    rt[s] = total[s].T
                theirs = st.at[i // 12, lax.rem(i // 4, 3), lax.rem(i, 4)]
                theirs[:, 0:64, :] = gt[i, :, pl.ds(their_rows, 64), :].astype(jnp.bfloat16)
                theirs[:, 64:128, :] = rt[:, pl.ds(their_rows, 64), :].astype(jnp.bfloat16)
                gt[i, :, pl.ds(their_rows, 64), :] = rt[:, pl.ds(mine_rows, 64), :]
                to_sibling(i).start()
                keep(i).start()
            return carry

        lax.fori_loop(0, ROWS, row, 0)

    for ring in tables:
        ring.start()
    for q in range(3):
        first(q).start()
    for ring in tables:
        ring.wait_recv()
    copy = pltpu.make_async_copy(tabv, tabs, tab_c)
    copy.start()
    copy.wait()
    for q in range(3):
        first(q).wait_recv()
        first(q + 3).start()
        stage(q)
        second(q).local().wait()
    for q in range(3):
        for delta in NEAR:
            second(q).arriving(delta).wait_recv()
        third(q).start()
        first(q + 3).wait_recv()
        second(q).wait_send()
        stage(q + 3)
        second(q + 3).local().wait()
    for q in range(3):
        for delta in NEAR:
            second(q + 3).arriving(delta).wait_recv()
        third(q + 3).start()
    for q in range(3):
        third(q).wait_recv()
    compute(0)
    for q in range(3):
        second(q + 3).wait_send()
    for q in range(3):
        third(q + 3).wait_recv()
    compute(1)
    for ring in tables:
        ring.wait_send()
    for p in range(PARTS):
        first(p).wait_send()
        third(p).wait_send()

    def drain(i, carry):
        to_sibling(i).wait()
        keep(i).wait()
        return carry

    lax.fori_loop(0, ROWS, drain, 0)


def mirror_kernel(
    own_ref, sib_ref, tab_ref, idx_ref,
    out_ref,
    ownv, sibv, ct,
    a0, a1, a2, b0, b1, b2, c0, c1, c2, d0, d1, d2,
    load, s1s, s1r, s2s, s2r, s3s, s3r,
):
    v, at, h = place()
    held = ((a0, b0, c0, d0), (a1, b1, c1, d1), (a2, b2, c2, d2))
    mine_rows = pl.multiple_of(h * 64, 64)
    one = pltpu.make_async_copy(own_ref.at[:, :, pl.ds(mine_rows, 64), :], ownv, load.at[0])
    two = pltpu.make_async_copy(sib_ref.at[:, :, pl.ds(0, 64), :], sibv, load.at[1])
    one.start()
    two.start()
    meet(v, at, h, False)
    one.wait()
    two.wait()

    def add(i, carry):
        ct[pl.ds(i * SLOTS, SLOTS)] = (ownv[i] + sibv[i].astype(jnp.float32)).astype(jnp.bfloat16)
        return carry

    lax.fori_loop(0, ROWS, add, 0)

    def rows_of(r):
        (f0, f1), (g0, g1) = CUTS[r]
        return f1 - f0, g1 - g0

    def first(r):
        return Ring(
            v, at, h, orders(r)[0],
            lambda there, delta: held[r][0].at[there],
            lambda mine: held[r][1].at[:, :, mine],
            lambda delta: s1s.at[r, delta],
            lambda mine: s1r.at[r, mine],
        )

    def second(r):
        return Ring(
            v, at, h, orders(r)[1],
            lambda there, delta: held[r][1].at[there],
            lambda mine: held[r][2].at[:, mine],
            lambda delta: s2s.at[r, delta],
            lambda mine: s2r.at[r, mine],
        )

    def third(r):
        return Ring(
            v, at, h, orders(r)[2],
            lambda there, delta: held[r][2].at[there],
            lambda mine: held[r][3].at[mine],
            lambda delta: s3s.at[r, delta],
            lambda mine: s3r.at[r, mine],
        )

    for r in range(3):
        a_axis, b_axis, c_axis = orders(r)
        (f0, f1), (g0, g1) = CUTS[r]
        n0, n1 = rows_of(r)

        def fill(n, carry):
            a, b = n // 4, lax.rem(n, 4)
            for c in range(4):
                target = a * STRIDES[a_axis] + b * STRIDES[b_axis] + c * STRIDES[c_axis]
                held[r][0][a, b, c, 0:n0, :] = ct[tab_ref[0, target], f0:f1, :]
                held[r][0][a, b, c, n0 : n0 + n1, :] = ct[tab_ref[1, target], g0:g1, :]
            return carry

        lax.fori_loop(0, 16, fill, 0)
        first(r).start()
    for r in range(3):
        first(r).wait_recv()
        second(r).start()
    for r in range(3):
        second(r).wait_recv()
        third(r).start()
    for r in range(3):
        third(r).wait_recv()

    def pick(i, carry):
        out_ref[i * SLOTS] = ct[i * SLOTS]
        for s in range(1, SLOTS):
            e = i * SLOTS + s
            both = []
            for r in range(3):
                n = idx_ref[r, e]
                c, b, a = lax.div(n, 32), lax.rem(lax.div(n, 8), 4), lax.rem(lax.div(n, 2), 4)
                both.append(held[r][3][c, b, a])
            low, high = [], []
            for r in range(3):
                n0, n1 = rows_of(r)
                low.append(both[r][0:n0, :])
                high.append(both[r][n0 : n0 + n1, :])
            use_high = jnp.full((64, LANES), lax.rem(idx_ref[0, e], 2), jnp.int32) > 0
            chosen = jnp.where(
                use_high,
                jnp.concatenate(high, axis=0).astype(jnp.float32),
                jnp.concatenate(low, axis=0).astype(jnp.float32),
            )
            out_ref[e] = chosen.astype(jnp.bfloat16)
        return carry

    lax.fori_loop(0, ROWS, pick, 0)
    for r in range(3):
        first(r).wait_send()
        second(r).wait_send()
        third(r).wait_send()


def end_kernel(scale, h_ref, own_ref, sib_ref, mirror_ref, om_ref, grad_ref, next_ref):
    rows = own_ref[0] + sib_ref[0].astype(jnp.float32)
    grad = (rows + mirror_ref[0].astype(jnp.float32)) * scale
    om = om_ref[0]
    at = (SLOTS, 64, BW)
    row = lax.broadcasted_iota(jnp.int32, at, 1) + h_ref[0] * 64
    diagonal = (row == lax.broadcasted_iota(jnp.int32, at, 2)) & (
        lax.broadcasted_iota(jnp.int32, at, 0) == 0
    )
    grad = grad - jnp.where(diagonal, 1.0 / jnp.where(diagonal, om, 1.0), 0.0)
    trial = om - STEP * grad
    edge = STEP * PENALTY
    shrunk = jnp.where(trial > edge, trial - edge, jnp.where(trial < -edge, trial + edge, 0.0))
    grad_ref[0] = grad
    next_ref[0] = jnp.where(diagonal, trial, shrunk)


def index_tables(block_cols):
    entry = jnp.arange(ENTRIES, dtype=jnp.int32)
    cols = block_cols.reshape(ENTRIES)
    owner = cols // ROWS
    slot = entry % SLOTS
    remote = slot != 0
    named = (owner[None, :] == jnp.arange(64, dtype=jnp.int32)[:, None]) & remote[None, :]
    low = jnp.min(jnp.where(named, entry[None, :], ENTRIES - 1), axis=1)
    high = jnp.max(jnp.where(named, entry[None, :], 0), axis=1)
    table = jnp.pad(jnp.stack([low, high]), ((0, 6), (0, 64)))
    key = (cols % ROWS) * SLOTS + slot
    before = (owner[:, None] == owner[None, :]) & remote[None, :] & (key[None, :] < key[:, None])
    second = jnp.any(before, axis=1).astype(jnp.int32)
    at = (owner // 16, (owner // 4) % 4, owner % 4)
    index = []
    for r in range(3):
        a, b, c = (at[axis] for axis in orders(r))
        index.append(((c * 4 + b) * 4 + a) * 2 + second)
    return table, jnp.stack(index)


def on_device(voxel_data, omega_blocks, block_cols):
    samples = voxel_data.shape[1] * lax.axis_size("samp")
    panels = voxel_data.reshape(ROWS, BW, voxel_data.shape[1])
    table, index = index_tables(block_cols)
    vmem, smem, hbm = pltpu.VMEM, pltpu.SMEM, pl.ANY
    bf16, f32, i32 = jnp.bfloat16, jnp.float32, jnp.int32
    dma = pltpu.SemaphoreType.DMA
    spec = pl.BlockSpec
    own, sib, _ = pl.pallas_call(
        panel_kernel,
        name="panel_exchange",
        out_shape=(
            jax.ShapeDtypeStruct((ROWS, SLOTS, BW, BW), f32),
            jax.ShapeDtypeStruct((ROWS, SLOTS, BW, BW), bf16),
            jax.ShapeDtypeStruct((PARTS, 4, 32, BW, LANES), bf16),
        ),
        in_specs=[
            spec(memory_space=hbm),
            spec(memory_space=hbm),
            spec(memory_space=vmem),
            spec(memory_space=smem),
        ],
        out_specs=(spec(memory_space=hbm),) * 3,
        scratch_shapes=[vmem((64, BW, LANES), bf16)] * PARTS
        + [vmem((128, BW, LANES), bf16)] * PARTS
        + [
            vmem((3, 3, 4, 8, BW, LANES), bf16),
            vmem((4, 8, BW, LANES), bf16),
            vmem((ROWS, SLOTS, BW, BW), f32),
            vmem((SLOTS * BW, 3 * LANES), bf16),
            vmem((2, SLOTS, BW, BW), f32),
            vmem((SLOTS, BW, BW), f32),
            vmem((3, 4, 8, 128), i32),
            smem((3, 4, 8, 128), i32),
            dma((3, 4)), dma((3, 4)), dma,
            dma((PARTS, 4)), dma((PARTS, 4)),
            dma((PARTS, 4)), dma((PARTS, 4)),
            dma((PARTS, 4)), dma((PARTS, 4)),
            dma((2,)), dma((ROWS,)), dma((ROWS,)), dma((ROWS,)),
        ],
        compiler_params=pltpu.CompilerParams(
            collective_id=0, has_side_effects=True, vmem_limit_bytes=63 << 20
        ),
    )(panels, omega_blocks, table, index)
    sizes = [sum(g1 - g0 for g0, g1 in CUTS[r]) for r in range(3)]
    mirror = pl.pallas_call(
        mirror_kernel,
        name="mirror_exchange",
        out_shape=jax.ShapeDtypeStruct((ENTRIES, 64, BW), bf16),
        in_specs=[
            spec(memory_space=hbm),
            spec(memory_space=hbm),
            spec(memory_space=smem),
            spec(memory_space=smem),
        ],
        out_specs=spec(memory_space=vmem),
        scratch_shapes=[
            vmem((ROWS, SLOTS, 64, BW), f32),
            vmem((ROWS, SLOTS, 64, BW), bf16),
            vmem((ENTRIES, 64, BW), bf16),
        ]
        + [vmem((4, 4, 4, n, BW), bf16) for n in sizes] * 4
        + [dma((2,))]
        + [dma((3, 4))] * 6,
        compiler_params=pltpu.CompilerParams(
            collective_id=1, has_side_effects=True, vmem_limit_bytes=40 << 20
        ),
    )(own, sib, table, index)
    h = lax.axis_index("samp").astype(i32).reshape(1)
    tile = (1, SLOTS, 64, BW)
    return pl.pallas_call(
        functools.partial(end_kernel, 0.5 / samples),
        name="proximal_end",
        out_shape=(jax.ShapeDtypeStruct((ROWS, SLOTS, 64, BW), f32),) * 2,
        grid_spec=pltpu.PrefetchScalarGridSpec(
            num_scalar_prefetch=1,
            grid=(ROWS,),
            in_specs=[
                spec(tile, lambda i, h_ref: (i, 0, 1 - h_ref[0], 0)),
                spec(tile, lambda i, h_ref: (i, 0, 1, 0)),
                spec(tile, lambda i, h_ref: (i, 0, 0, 0)),
                spec(tile, lambda i, h_ref: (i, 0, h_ref[0], 0)),
            ],
            out_specs=(spec(tile, lambda i, h_ref: (i, 0, 0, 0)),) * 2,
        ),
    )(h, own, sib, mirror.reshape(ROWS, SLOTS, 64, BW), omega_blocks)


def solution(mesh):
    in_specs = (P("vars", "samp"), P("vars", None, None, None), P("vars", None))
    out_specs = (P("vars", None, "samp", None), P("vars", None, "samp", None))
    return jax.shard_map(
        on_device, mesh=mesh, in_specs=in_specs, out_specs=out_specs, check_vma=False
    )
```

```python
import jax
import jax.numpy as jnp
from jax import lax
from jax.experimental import pallas as pl
from jax.experimental.pallas import tpu as pltpu
from jax.sharding import PartitionSpec as P

STEP = 0.5
PENALTY = 0.1
MESH = pl.DeviceIdType.MESH
RING = 4
STRIDES = (16, 4, 1)
BW = 128
ROWS = 16
SLOTS = 8
ENTRIES = ROWS * SLOTS
LANES = 128
PARTS = 6
NEAR = (1, 3, 2)
CUTS = (((0, 16), (0, 16)), ((16, 32), (16, 48)), ((32, 64), (48, 64)))


def place():
    v = lax.axis_index("vars")
    at = (v // 16, lax.rem(v // 4, RING), lax.rem(v, RING))
    return v, at, lax.axis_index("samp")


def orders(r):
    return r % 3, (r + 1) % 3, (r + 2) % 3


def moved(v, at, axis, delta):
    there = lax.rem(at[axis] + delta, RING)
    return there, v + (there - at[axis]) * STRIDES[axis]


def greet(v, at, h, semaphore):
    for axis in range(3):
        for delta in NEAR:
            pl.semaphore_signal(
                semaphore, inc=1, device_id=(moved(v, at, axis, delta)[1], h), device_id_type=MESH
            )
    pl.semaphore_signal(semaphore, inc=1, device_id=(v, 1 - h), device_id_type=MESH)


def split(n):
    return lax.div(n, 32), lax.rem(lax.div(n, 8), 4), lax.rem(lax.div(n, 2), 4), lax.rem(n, 2)


class Ring:
    def __init__(self, v, at, h, axis, source, landing, send, recv):
        self.v, self.at, self.h, self.axis = v, at, h, axis
        self.source, self.landing, self.send, self.recv = source, landing, send, recv

    def remote(self, delta):
        there, target = moved(self.v, self.at, self.axis, delta)
        mine = self.at[self.axis]
        return pltpu.make_async_remote_copy(
            src_ref=self.source(there, delta),
            dst_ref=self.landing(mine),
            send_sem=self.send(delta),
            recv_sem=self.recv(mine),
            device_id=(target, self.h),
            device_id_type=MESH,
        )

    def arriving(self, delta):
        there, target = moved(self.v, self.at, self.axis, delta)
        return pltpu.make_async_remote_copy(
            src_ref=self.source(there, delta),
            dst_ref=self.landing(there),
            send_sem=self.send(delta),
            recv_sem=self.recv(there),
            device_id=(target, self.h),
            device_id_type=MESH,
        )

    def local(self):
        mine = self.at[self.axis]
        return pltpu.make_async_copy(self.source(mine, 0), self.landing(mine), self.recv(mine))

    def start(self):
        for delta in NEAR:
            self.remote(delta).start()
        self.local().start()

    def wait_recv(self):
        for delta in NEAR:
            self.arriving(delta).wait_recv()
        self.local().wait()

    def wait_send(self):
        for delta in NEAR:
            self.remote(delta).wait_send()


def step_kernel(
    x_ref, om_ref, tab_ref, idx_ref,
    out_ref, s2_ref,
    ag0, ag1, ag2, ag3, ag4, ag5,
    fin0, fin1, fin2, fin3, fin4, fin5,
    st, sto, gt, xc, omv, rt, ct, tabv, tabs,
    tab_s, tab_r, tab_c, s1s, s1r, s1l, s2s, s2r, s3s, s3r,
    om_sem, out_sem, sib_s, sib_r, m1s, m1r, m2s, m2r, m3s, m3r, free,
):
    v, at, h = place()
    ag = (ag0, ag1, ag2, ag3, ag4, ag5)
    fin = (fin0, fin1, fin2, fin3, fin4, fin5)
    greet(v, at, h, pltpu.get_barrier_semaphore())
    pl.semaphore_wait(pltpu.get_barrier_semaphore(), 10)

    tables = [
        Ring(
            v, at, h, axis,
            lambda there, delta: tab_ref,
            lambda mine, axis=axis: tabv.at[axis, mine],
            lambda delta, axis=axis: tab_s.at[axis, delta],
            lambda mine, axis=axis: tab_r.at[axis, mine],
        )
        for axis in range(3)
    ]

    def hand_on(p, delta, second_leg):
        axis = orders(p)[0]
        slot = (0 if delta == 1 else 1) + (2 if second_leg else 0)
        _, target = moved(v, at, axis, delta)
        if second_leg:
            origin = lax.rem(at[axis] + (RING - delta), RING)
            rows = pl.ds(origin * ROWS + (0 if delta == 1 else 8), 8)
            source = ag[p].at[rows]
        else:
            rows = pl.ds(at[axis] * ROWS, ROWS)
            source = x_ref.at[:, :, pl.ds(p * LANES, LANES)]
        return pltpu.make_async_remote_copy(
            src_ref=source,
            dst_ref=ag[p].at[rows],
            send_sem=s1s.at[p, slot],
            recv_sem=s1r.at[p, slot],
            device_id=(target, h),
            device_id_type=MESH,
        )

    def handed(p, delta, second_leg):
        axis = orders(p)[0]
        slot = (0 if delta == 1 else 1) + (2 if second_leg else 0)
        _, target = moved(v, at, axis, delta)
        origin = lax.rem(at[axis] + (RING - delta) * (2 if second_leg else 1), RING)
        if second_leg:
            rows = pl.ds(origin * ROWS + (0 if delta == 1 else 8), 8)
        else:
            rows = pl.ds(origin * ROWS, ROWS)
        return pltpu.make_async_remote_copy(
            src_ref=ag[p].at[rows],
            dst_ref=ag[p].at[rows],
            send_sem=s1s.at[p, slot],
            recv_sem=s1r.at[p, slot],
            device_id=(target, h),
            device_id_type=MESH,
        )

    def own_panels(p):
        return pltpu.make_async_copy(
            x_ref.at[:, :, pl.ds(p * LANES, LANES)],
            ag[p].at[pl.ds(at[orders(p)[0]] * ROWS, ROWS)],
            s1l.at[p],
        )

    def first_start(p):
        hand_on(p, 1, False).start()
        hand_on(p, 3, False).start()
        own_panels(p).start()

    def first_turn(p):
        for delta in (1, 3):
            handed(p, delta, False).wait_recv()
            hand_on(p, delta, True).start()

    def first_wait(p):
        for delta in (1, 3):
            handed(p, delta, True).wait_recv()
        own_panels(p).wait()

    def second(p):
        return Ring(
            v, at, h, orders(p)[1],
            lambda there, delta: st.at[p % 3, delta - 1] if delta else sto,
            lambda mine: s2_ref.at[p, :, mine],
            lambda delta: s2s.at[p, delta],
            lambda mine: s2r.at[p, mine],
        )

    def third(p):
        return Ring(
            v, at, h, orders(p)[2],
            lambda there, delta: s2_ref.at[p, there],
            lambda mine: fin[p].at[mine],
            lambda delta: s3s.at[p, delta],
            lambda mine: s3r.at[p, mine],
        )

    def stage(p):
        a_axis, b_axis, c_axis = orders(p)
        ring = second(p)
        for delta in (1, 3, 2, 0):
            there = lax.rem(at[b_axis] + delta, RING)
            base = at[a_axis] * STRIDES[a_axis] + there * STRIDES[b_axis]
            held = st.at[p % 3, delta - 1] if delta else sto

            def fill(c, carry):
                target = base + c * STRIDES[c_axis]
                for a in range(4):
                    for k in range(2):
                        entry = tabs[a_axis, a, k, target]
                        held[c, a, k] = ag[p][a * ROWS + lax.div(entry, SLOTS)]
                return carry

            lax.fori_loop(0, RING, fill, 0)
            if delta:
                ring.remote(delta).start()
            else:
                ring.local().start()

    def omega(i, slot):
        return pltpu.make_async_copy(om_ref.at[i], omv.at[slot], om_sem.at[slot])

    def to_sibling(i):
        return pltpu.make_async_remote_copy(
            src_ref=st.at[i // 12, lax.rem(i // 4, 3), lax.rem(i, 4)],
            dst_ref=fin0.at[i // 4, lax.rem(i, 4)],
            send_sem=sib_s.at[i],
            recv_sem=sib_r.at[i],
            device_id=(v, 1 - h),
            device_id_type=MESH,
        )

    mine_rows = pl.multiple_of(h * 64, 64)
    their_rows = pl.multiple_of((1 - h) * 64, 64)

    def compute(group):
        omega(0, 0).start()

        def row(i, carry):
            slot = lax.rem(i, 2)
            omega(i, slot).wait()

            @pl.when(i + 1 < ROWS)
            def _():
                omega(i + 1, 1 - slot).start()

            for q in range(3):
                p = group * 3 + q
                cols = pl.ds(q * LANES, LANES)
                xc[0:BW, cols] = ag[p][at[orders(p)[0]] * ROWS + i]
                for s in range(1, SLOTS):
                    c, b, a, k = split(idx_ref[q, i * SLOTS + s])
                    xc[s * BW : (s + 1) * BW, cols] = fin[p][c, b, a, k]
            blocks = omv[slot].astype(jnp.bfloat16)
            lhs = jnp.concatenate([blocks[s] for s in range(SLOTS)], axis=1)
            w = jnp.dot(lhs, xc[...], preferred_element_type=jnp.float32).astype(jnp.bfloat16)
            turned = lax.dot_general(
                xc[...], w, (((1,), (1,)), ((), ())), preferred_element_type=jnp.float32
            ).reshape(SLOTS, BW, BW)
            if group == 0:
                gt[i] = turned
            else:
                total = gt[i] + turned
                gt[i] = total
                for s in range(SLOTS):
                    rt[s] = total[s].T
                theirs = st.at[i // 12, lax.rem(i // 4, 3), lax.rem(i, 4)]
                pairs = (4, 2, 64, BW)
                columns = gt[i, :, pl.ds(their_rows, 64), :].astype(jnp.bfloat16)
                theirs[:, :, 0:64, :] = columns.reshape(pairs)
                rows = rt[:, pl.ds(their_rows, 64), :].astype(jnp.bfloat16)
                theirs[:, :, 64:128, :] = rows.reshape(pairs)
                gt[i, :, pl.ds(their_rows, 64), :] = rt[:, pl.ds(mine_rows, 64), :]
                to_sibling(i).start()
            return carry

        lax.fori_loop(0, ROWS, row, 0)

    for q in range(3):
        first_start(q)
    for ring in tables:
        ring.start()
    for q in range(3):
        first_turn(q)
        first_start(q + 3)
    for ring in tables:
        ring.wait_recv()
    copy = pltpu.make_async_copy(tabv, tabs, tab_c)
    copy.start()
    copy.wait()
    for q in range(3):
        first_wait(q)
        stage(q)
        second(q).local().wait()
    for q in range(3):
        first_turn(q + 3)
    for q in range(3):
        for delta in NEAR:
            second(q).arriving(delta).wait_recv()
        third(q).start()
        first_wait(q + 3)
        second(q).wait_send()
        stage(q + 3)
        second(q + 3).local().wait()
    for q in range(3):
        for delta in NEAR:
            second(q + 3).arriving(delta).wait_recv()
        third(q + 3).start()
    for q in range(3):
        third(q).wait_recv()
    compute(0)
    greet(v, at, h, free)
    for q in range(3):
        second(q + 3).wait_send()
    pl.semaphore_wait(free, 10)
    for q in range(3):
        third(q + 3).wait_recv()
    compute(1)

    def add(i, carry):
        to_sibling(i).wait_recv()
        mine = gt[i, :, pl.ds(mine_rows, 64), :]
        theirs = fin0[i // 4, lax.rem(i, 4), :, :, 0:64, :].reshape(SLOTS, 64, BW)
        ct[pl.ds(i * SLOTS, SLOTS)] = (mine + theirs.astype(jnp.float32)).astype(jnp.bfloat16)
        return carry

    lax.fori_loop(0, ROWS, add, 0)

    def cut(r):
        (f0, f1), (g0, g1) = CUTS[r]
        return f0, f1, g0, g1, f0 + g0, f1 - f0, g1 - g0

    def piece(r):
        _, _, _, _, start, n0, n1 = cut(r)
        return slice(start, start + n0 + n1)

    def back_first(r):
        return Ring(
            v, at, h, orders(r)[0],
            lambda there, delta: fin2.at[there, :, :, 1, piece(r), :],
            lambda mine: fin1.at[:, :, mine, 0, piece(r), :],
            lambda delta: m1s.at[r, delta],
            lambda mine: m1r.at[r, mine],
        )

    def back_second(r):
        return Ring(
            v, at, h, orders(r)[1],
            lambda there, delta: fin1.at[there, :, :, 0, piece(r), :],
            lambda mine: fin1.at[:, mine, :, 1, piece(r), :],
            lambda delta: m2s.at[r, delta],
            lambda mine: m2r.at[r, mine],
        )

    def back_third(r):
        return Ring(
            v, at, h, orders(r)[2],
            lambda there, delta: fin1.at[there, :, :, 1, piece(r), :],
            lambda mine: fin2.at[mine, :, :, 0, piece(r), :],
            lambda delta: m3s.at[r, delta],
            lambda mine: m3r.at[r, mine],
        )

    for r in range(3):
        a_axis, b_axis, c_axis = orders(r)
        f0, f1, g0, g1, start, n0, n1 = cut(r)

        def fill(n, carry):
            a, b = n // 4, lax.rem(n, 4)
            for c in range(4):
                target = a * STRIDES[a_axis] + b * STRIDES[b_axis] + c * STRIDES[c_axis]
                low, high = tabs[0, at[0], 0, target], tabs[0, at[0], 1, target]
                fin2[a, b, c, 1, start : start + n0, :] = ct[low, f0:f1, :]
                fin2[a, b, c, 1, start + n0 : start + n0 + n1, :] = ct[high, g0:g1, :]
            return carry

        lax.fori_loop(0, 16, fill, 0)
        back_first(r).start()

    def settle(i, carry):
        theirs = fin0[i // 4, lax.rem(i, 4), :, :, 64:128, :].reshape(SLOTS, 64, BW)
        gt[i, :, pl.ds(their_rows, 64), :] += theirs.astype(jnp.float32)
        return carry

    lax.fori_loop(0, ROWS, settle, 0)
    for r in range(3):
        back_first(r).wait_recv()
        back_second(r).start()
    for r in range(3):
        back_second(r).wait_recv()
        back_third(r).start()
    for r in range(3):
        back_third(r).wait_recv()

    def result(i):
        return pltpu.make_async_copy(
            gt.at[i, :, pl.ds(their_rows, 64), :], out_ref.at[i], out_sem.at[i]
        )

    def pick(i, carry):
        gt[i, 0, pl.ds(their_rows, 64), :] += ct[i * SLOTS].astype(jnp.float32)
        for s in range(1, SLOTS):
            e = i * SLOTS + s
            low, high = [], []
            for r in range(3):
                _, _, _, _, start, n0, n1 = cut(r)
                c, b, a, k = split(idx_ref[r, e])
                low.append(fin2[c, b, a, 0, start : start + n0, :])
                high.append(fin2[c, b, a, 0, start + n0 : start + n0 + n1, :])
            use_high = jnp.full((64, LANES), k, jnp.int32) > 0
            gt[i, s, pl.ds(their_rows, 64), :] += jnp.where(
                use_high,
                jnp.concatenate(high, axis=0).astype(jnp.float32),
                jnp.concatenate(low, axis=0).astype(jnp.float32),
            )
        result(i).start()
        return carry

    lax.fori_loop(0, ROWS, pick, 0)
    for ring in tables:
        ring.wait_send()
    for p in range(PARTS):
        for delta in (1, 3):
            hand_on(p, delta, False).wait_send()
            hand_on(p, delta, True).wait_send()
        third(p).wait_send()
    for r in range(3):
        back_first(r).wait_send()
        back_second(r).wait_send()
        back_third(r).wait_send()

    def drain(i, carry):
        to_sibling(i).wait_send()
        result(i).wait()
        return carry

    lax.fori_loop(0, ROWS, drain, 0)


def index_tables(block_cols):
    entry = jnp.arange(ENTRIES, dtype=jnp.int32)
    cols = block_cols.reshape(ENTRIES)
    owner = cols // ROWS
    slot = entry % SLOTS
    remote = slot != 0
    named = (owner[None, :] == jnp.arange(64, dtype=jnp.int32)[:, None]) & remote[None, :]
    low = jnp.min(jnp.where(named, entry[None, :], ENTRIES - 1), axis=1)
    high = jnp.max(jnp.where(named, entry[None, :], 0), axis=1)
    table = jnp.pad(jnp.stack([low, high]), ((0, 6), (0, 64)))
    key = (cols % ROWS) * SLOTS + slot
    before = (owner[:, None] == owner[None, :]) & remote[None, :] & (key[None, :] < key[:, None])
    second = jnp.any(before, axis=1).astype(jnp.int32)
    at = (owner // 16, (owner // 4) % 4, owner % 4)
    index = []
    for r in range(3):
        a, b, c = (at[axis] for axis in orders(r))
        index.append(((c * 4 + b) * 4 + a) * 2 + second)
    return table, jnp.stack(index)


def on_device(voxel_data, omega_blocks, block_cols):
    samples = voxel_data.shape[1] * lax.axis_size("samp")
    panels = voxel_data.reshape(ROWS, BW, voxel_data.shape[1])
    table, index = index_tables(block_cols)
    vmem, smem, hbm = pltpu.VMEM, pltpu.SMEM, pl.ANY
    bf16, f32, i32 = jnp.bfloat16, jnp.float32, jnp.int32
    dma = pltpu.SemaphoreType.DMA
    spec = pl.BlockSpec
    combined, _ = pl.pallas_call(
        step_kernel,
        name="concord_exchange",
        out_shape=(
            jax.ShapeDtypeStruct((ROWS, SLOTS, 64, BW), f32),
            jax.ShapeDtypeStruct((PARTS, 4, 4, 4, 2, BW, LANES), bf16),
        ),
        in_specs=[
            spec(memory_space=hbm),
            spec(memory_space=hbm),
            spec(memory_space=vmem),
            spec(memory_space=smem),
        ],
        out_specs=(spec(memory_space=hbm),) * 2,
        scratch_shapes=[vmem((64, BW, LANES), bf16)] * PARTS
        + [vmem((4, 4, 4, 2, BW, LANES), bf16)] * PARTS
        + [
            vmem((3, 3, 4, 4, 2, BW, LANES), bf16),
            vmem((4, 4, 2, BW, LANES), bf16),
            vmem((ROWS, SLOTS, BW, BW), f32),
            vmem((SLOTS * BW, 3 * LANES), bf16),
            vmem((2, SLOTS, BW, BW), f32),
            vmem((SLOTS, BW, BW), f32),
            vmem((ENTRIES, 64, BW), bf16),
            vmem((3, 4, 8, 128), i32),
            smem((3, 4, 8, 128), i32),
            dma((3, 4)), dma((3, 4)), dma,
            dma((PARTS, 4)), dma((PARTS, 4)), dma((PARTS,)),
            dma((PARTS, 4)), dma((PARTS, 4)),
            dma((PARTS, 4)), dma((PARTS, 4)),
            dma((2,)), dma((ROWS,)), dma((ROWS,)), dma((ROWS,)),
            dma((3, 4)), dma((3, 4)), dma((3, 4)), dma((3, 4)), dma((3, 4)), dma((3, 4)),
            pltpu.SemaphoreType.REGULAR,
        ],
        compiler_params=pltpu.CompilerParams(
            collective_id=0, has_side_effects=True, vmem_limit_bytes=63 << 20
        ),
    )(panels, omega_blocks, table, index)
    start = lax.axis_index("samp") * 64
    om = lax.dynamic_slice_in_dim(omega_blocks, start, 64, 2)
    at = (1, SLOTS, 64, BW)
    row = lax.broadcasted_iota(jnp.int32, at, 2) + start
    diagonal = (row == lax.broadcasted_iota(jnp.int32, at, 3)) & (
        lax.broadcasted_iota(jnp.int32, at, 1) == 0
    )
    gradient = combined * (0.5 / samples) - jnp.where(
        diagonal, 1.0 / jnp.where(diagonal, om, 1.0), 0.0
    )
    trial = om - STEP * gradient
    shrunk = jnp.sign(trial) * jnp.maximum(jnp.abs(trial) - STEP * PENALTY, 0.0)
    return gradient, jnp.where(diagonal, trial, shrunk)


def solution(mesh):
    in_specs = (P("vars", "samp"), P("vars", None, None, None), P("vars", None))
    out_specs = (P("vars", None, "samp", None), P("vars", None, "samp", None))
    return jax.shard_map(
        on_device, mesh=mesh, in_specs=in_specs, out_specs=out_specs, check_vma=False
    )
```

```python
import functools

import jax
import jax.numpy as jnp
from jax import lax
from jax.experimental import pallas as pl
from jax.experimental.pallas import tpu as pltpu
from jax.sharding import PartitionSpec as P

STEP = 0.5
PENALTY = 0.1
MESH = pl.DeviceIdType.MESH
RING = 4
STRIDES = (16, 4, 1)
BW = 128
ROWS = 16
SLOTS = 8
ENTRIES = ROWS * SLOTS
LANES = 128
PARTS = 6
PIECES = (((0, 32), (32, 80), (80, 128)), ((0, 48), (48, 80), (80, 128)), ((0, 48), (48, 96), (96, 128)))
GROUPS = ((0, 1, 2), (3, 4), (5,))
END_ROWS = 4
NEAR = (1, 3, 2)
CUTS = (((0, 16), (0, 16)), ((16, 32), (16, 48)), ((32, 64), (48, 64)))


def place():
    v = lax.axis_index("vars")
    at = (v // 16, lax.rem(v // 4, RING), lax.rem(v, RING))
    return v, at, lax.axis_index("samp")


def orders(r):
    return r % 3, (r + 1) % 3, (r + 2) % 3


def moved(v, at, axis, delta):
    there = lax.rem(at[axis] + delta, RING)
    return there, v + (there - at[axis]) * STRIDES[axis]


def greet(v, at, h, semaphore):
    for axis in range(3):
        for delta in NEAR:
            pl.semaphore_signal(
                semaphore, inc=1, device_id=(moved(v, at, axis, delta)[1], h), device_id_type=MESH
            )
    pl.semaphore_signal(semaphore, inc=1, device_id=(v, 1 - h), device_id_type=MESH)


def split(idx_ref, r, e):
    a, b, c = orders(r)
    return idx_ref[c, e], idx_ref[b, e], idx_ref[a, e], idx_ref[3, e]


class Ring:
    def __init__(self, v, at, h, axis, source, landing, send, recv):
        self.v, self.at, self.h, self.axis = v, at, h, axis
        self.source, self.landing, self.send, self.recv = source, landing, send, recv

    def remote(self, delta):
        there, target = moved(self.v, self.at, self.axis, delta)
        mine = self.at[self.axis]
        return pltpu.make_async_remote_copy(
            src_ref=self.source(there, delta),
            dst_ref=self.landing(mine),
            send_sem=self.send(delta),
            recv_sem=self.recv(mine),
            device_id=(target, self.h),
            device_id_type=MESH,
        )

    def arriving(self, delta):
        there, target = moved(self.v, self.at, self.axis, delta)
        return pltpu.make_async_remote_copy(
            src_ref=self.source(there, delta),
            dst_ref=self.landing(there),
            send_sem=self.send(delta),
            recv_sem=self.recv(there),
            device_id=(target, self.h),
            device_id_type=MESH,
        )

    def local(self):
        mine = self.at[self.axis]
        return pltpu.make_async_copy(self.source(mine, 0), self.landing(mine), self.recv(mine))

    def start(self):
        for delta in NEAR:
            self.remote(delta).start()
        self.local().start()

    def wait_recv(self):
        for delta in NEAR:
            self.arriving(delta).wait_recv()
        self.local().wait()

    def wait_send(self):
        for delta in NEAR:
            self.remote(delta).wait_send()


def step_kernel(
    weight,
    x_ref, om_ref, tab_ref, idx_ref,
    out_ref, s2_ref,
    ag0, ag1, ag2, ag3, ag4, ag5,
    fin0, fin1, fin2, fin3, fin4, fin5,
    st, sto, gt, xc, omv, rt, ct, dm, tabv, tabs,
    tab_s, tab_r, tab_c, s1s, s1r, s1l, s2s, s2r, s3s, s3r,
    om_sem, dm_sem, out_sem, sib_s, sib_r, back_s, back_r, free,
):
    v, at, h = place()
    ag = (ag0, ag1, ag2, ag3, ag4, ag5)
    fin = (fin0, fin1, fin2, fin3, fin4, fin5)
    greet(v, at, h, pltpu.get_barrier_semaphore())
    pl.semaphore_wait(pltpu.get_barrier_semaphore(), 10)

    tables = [
        Ring(
            v, at, h, axis,
            lambda there, delta: tab_ref,
            lambda mine, axis=axis: tabv.at[axis, mine],
            lambda delta, axis=axis: tab_s.at[axis, delta],
            lambda mine, axis=axis: tab_r.at[axis, mine],
        )
        for axis in range(3)
    ]

    def piece(p, r):
        low, high = PIECES[p % 3][r]
        return slice(low, high)

    def leg_of(p, r, delta, second_leg, arriving):
        axis = orders(r)[0]
        slot = (0 if delta == 1 else 1) + (2 if second_leg else 0)
        _, target = moved(v, at, axis, delta)
        back = RING - delta
        origin = lax.rem(at[axis] + back * (int(second_leg) + int(arriving)), RING)
        if second_leg:
            rows = pl.ds(origin * ROWS + (0 if delta == 1 else 8), 8)
        else:
            rows = pl.ds(origin * ROWS, ROWS)
        landing = ag[p].at[rows, piece(p, r)]
        if second_leg or arriving:
            source = landing
        else:
            source = x_ref.at[:, piece(p, r), pl.ds(p * LANES, LANES)]
        return pltpu.make_async_remote_copy(
            src_ref=source,
            dst_ref=landing,
            send_sem=s1s.at[p, r, slot],
            recv_sem=s1r.at[p, r, slot],
            device_id=(target, h),
            device_id_type=MESH,
        )

    def own_panels(p, r):
        return pltpu.make_async_copy(
            x_ref.at[:, piece(p, r), pl.ds(p * LANES, LANES)],
            ag[p].at[pl.ds(at[orders(r)[0]] * ROWS, ROWS), piece(p, r)],
            s1l.at[p, r],
        )

    def first_start(p):
        for r in range(3):
            leg_of(p, r, 1, False, False).start()
            leg_of(p, r, 3, False, False).start()
        for r in range(3):
            own_panels(p, r).start()

    def first_turn(p):
        for r in range(3):
            for delta in (1, 3):
                leg_of(p, r, delta, False, True).wait_recv()
                leg_of(p, r, delta, True, False).start()

    def first_sent(p):
        for r in range(3):
            for delta in (1, 3):
                for second_leg in (False, True):
                    leg_of(p, r, delta, second_leg, False).wait_send()

    def first_wait(p, r):
        for delta in (1, 3):
            leg_of(p, r, delta, True, True).wait_recv()
        own_panels(p, r).wait()

    def second(p, r):
        rows = piece(p, r)
        return Ring(
            v, at, h, orders(r)[1],
            lambda there, delta: (
                st.at[p % 3, delta - 1, :, :, :, rows] if delta else sto.at[:, :, :, rows]
            ),
            lambda mine: s2_ref.at[p, :, mine, :, :, rows],
            lambda delta: s2s.at[p, r, delta],
            lambda mine: s2r.at[p, r, mine],
        )

    def third(p, r):
        rows = piece(p, r)
        return Ring(
            v, at, h, orders(r)[2],
            lambda there, delta: s2_ref.at[p, there, :, :, :, rows],
            lambda mine: fin[p].at[mine, :, :, :, rows],
            lambda delta: s3s.at[p, r, delta],
            lambda mine: s3r.at[p, r, mine],
        )

    def stage(p, r):
        a_axis, b_axis, c_axis = orders(r)
        ring = second(p, r)
        rows = piece(p, r)
        for delta in (1, 3, 2, 0):
            there = lax.rem(at[b_axis] + delta, RING)
            base = at[a_axis] * STRIDES[a_axis] + there * STRIDES[b_axis]
            held = st.at[p % 3, delta - 1] if delta else sto

            def fill(c, carry):
                target = base + c * STRIDES[c_axis]
                for a in range(4):
                    for k in range(2):
                        row = a * ROWS + tabs[a_axis, a, 2 + k, target]
                        held[c, a, k, rows, :] = ag[p][row, rows, :]
                return carry

            lax.fori_loop(0, RING, fill, 0)
            if delta:
                ring.remote(delta).start()
            else:
                ring.local().start()

    def second_start(p):
        if p >= 3:
            for r in range(3):
                second(p - 3, r).wait_send()
        for r in range(3):
            first_wait(p, r)
        for r in range(3):
            stage(p, r)
        for r in range(3):
            second(p, r).local().wait()

    def third_start(p):
        for r in range(3):
            for delta in NEAR:
                second(p, r).arriving(delta).wait_recv()
            third(p, r).start()

    def third_wait(p):
        for r in range(3):
            third(p, r).wait_recv()

    def omega(i, slot):
        return pltpu.make_async_copy(om_ref.at[i], omv.at[slot], om_sem.at[slot])

    def to_sibling(i):
        return pltpu.make_async_remote_copy(
            src_ref=st.at[i // 12, lax.rem(i // 4, 3), lax.rem(i, 4)],
            dst_ref=fin0.at[i // 4, lax.rem(i, 4)],
            send_sem=sib_s.at[i],
            recv_sem=sib_r.at[i],
            device_id=(v, 1 - h),
            device_id_type=MESH,
        )

    mine_rows = pl.multiple_of(h * 64, 64)
    their_rows = pl.multiple_of((1 - h) * 64, 64)

    def kept(j, n):
        return ag[n].at[pl.ds(j * SLOTS, SLOTS)]

    def compute(group):
        if group < 2:
            for n in range(2):
                omega(n, n).start()

        width = len(GROUPS[group]) * LANES

        def pair(j, carry):
            held = []
            for n in range(2):
                i = j * 2 + n
                for q, p in enumerate(GROUPS[group]):
                    cols = slice(q * LANES, (q + 1) * LANES)
                    for r in range(3):
                        rows = piece(p, r)
                        own = at[orders(r)[0]] * ROWS + i
                        xc[n, rows, cols] = ag[p][own, rows, :]
                    for s in range(1, SLOTS):
                        for r in range(3):
                            low, high = PIECES[p % 3][r]
                            c, b, a, k = split(idx_ref, r, i * SLOTS + s)
                            xc[n, s * BW + low : s * BW + high, cols] = fin[p][
                                c, b, a, k, low:high, :
                            ]
                if group < 2:
                    slot = lax.rem(j, 2) * 2 + n
                    omega(i, slot).wait()

                    @pl.when(j + 1 < ROWS // 2)
                    def _():
                        omega(i + 2, (1 - lax.rem(j, 2)) * 2 + n).start()

                    blocks = omv[slot].astype(jnp.bfloat16)
                    if group == 1:
                        kept(j, n)[...] = blocks
                else:
                    blocks = kept(j, n)[...]
                held.append(jnp.concatenate([blocks[s] for s in range(SLOTS)], axis=1))
            w = [
                jnp.dot(held[n], xc[n, :, 0:width], preferred_element_type=jnp.float32).astype(jnp.bfloat16)
                for n in range(2)
            ]
            for n in range(2):
                i = j * 2 + n
                turned = lax.dot_general(
                    xc[n, :, 0:width], w[n], (((1,), (1,)), ((), ())), preferred_element_type=jnp.float32
                ).reshape(SLOTS, BW, BW)
                if group == 0:
                    gt[i] = turned
                elif group < len(GROUPS) - 1:
                    gt[i] += turned
                else:
                    total = gt[i] + turned
                    gt[i] = total
                    theirs = st.at[i // 12, lax.rem(i // 4, 3), lax.rem(i, 4)]
                    theirs[...] = total.astype(jnp.bfloat16).reshape(4, 2, BW, BW)
                    to_sibling(i).start()
            return carry

        lax.fori_loop(0, ROWS // 2, pair, 0)

    diagonals = pltpu.make_async_copy(om_ref.at[:, 0, pl.ds(mine_rows, 64), :], dm, dm_sem)
    diagonals.start()
    first_start(0)
    for ring in tables:
        ring.start()
    first_start(1)
    first_turn(0)
    first_start(2)
    first_turn(1)
    for ring in tables:
        ring.wait_recv()
    copy = pltpu.make_async_copy(tabv, tabs, tab_c)
    copy.start()
    copy.wait()
    second_start(0)
    first_start(3)
    first_turn(2)
    second_start(1)
    first_start(4)
    first_turn(3)
    third_start(0)
    second_start(2)
    first_start(5)
    first_turn(4)
    third_start(1)
    second_start(3)
    first_turn(5)
    third_start(2)
    second_start(4)
    third_start(3)
    for p in range(3):
        third_wait(p)
    second_start(5)
    compute(0)
    greet(v, at, h, free)
    third_start(4)
    third_start(5)
    third_wait(3)
    third_wait(4)
    for p in range(2):
        first_sent(p)
    compute(1)
    for p in range(3, 6):
        for r in range(3):
            second(p, r).wait_send()
    pl.semaphore_wait(free, 10)
    third_wait(5)
    compute(2)

    def add(i, carry):
        to_sibling(i).wait_recv()
        mine = gt[i, :, pl.ds(mine_rows, 64), :]
        theirs = fin0[i // 4, lax.rem(i, 4), :, :, pl.ds(mine_rows, 64), :].reshape(SLOTS, 64, BW)
        ct[pl.ds(i * SLOTS, SLOTS)] = (mine + theirs.astype(jnp.float32)).astype(jnp.bfloat16)
        return carry

    lax.fori_loop(0, ROWS, add, 0)

    def cut(r, u):
        low, high = CUTS[r][u]
        start = sum(pair[0][1] - pair[0][0] + pair[1][1] - pair[1][0] for pair in CUTS[:r])
        start += (CUTS[r][0][1] - CUTS[r][0][0]) * u
        return low, high, start, start + high - low

    def back(leg, r, u):
        rows = slice(*cut(r, u)[2:])
        source = (
            lambda there, delta: fin2.at[there, :, :, 1, rows, :],
            lambda there, delta: fin1.at[there, :, :, 0, rows, :],
            lambda there, delta: fin1.at[there, :, :, 1, rows, :],
        )
        landing = (
            lambda mine: fin1.at[:, :, mine, 0, rows, :],
            lambda mine: fin1.at[:, mine, :, 1, rows, :],
            lambda mine: fin2.at[mine, :, :, 0, rows, :],
        )
        return Ring(
            v, at, h, orders(r)[leg], source[leg], landing[leg],
            lambda delta: back_s.at[leg, r * 2 + u, delta],
            lambda mine: back_r.at[leg, r * 2 + u, mine],
        )

    for u in range(2):
        for r in range(3):
            a_axis, b_axis, c_axis = orders(r)
            low, high, start, end = cut(r, u)

            def fill(n, carry):
                a, b = n // 4, lax.rem(n, 4)
                for c in range(4):
                    target = a * STRIDES[a_axis] + b * STRIDES[b_axis] + c * STRIDES[c_axis]
                    entry = tabs[0, at[0], u, target]
                    fin2[a, b, c, 1, start:end, :] = ct[entry, low:high, :]
                return carry

            lax.fori_loop(0, 16, fill, 0)
            back(0, r, u).start()

    on_diagonal = lax.broadcasted_iota(jnp.int32, (64, BW), 0) + mine_rows == (
        lax.broadcasted_iota(jnp.int32, (64, BW), 1)
    )
    diagonals.wait()

    def settle(i, carry):
        for s in range(SLOTS):
            theirs = fin0[i // 4, lax.rem(i, 4), s // 2, s % 2].astype(jnp.float32)
            rt[s] = (gt[i, s] + theirs).T
        gt[i, :, pl.ds(their_rows, 64), :] = rt[:, pl.ds(mine_rows, 64), :]
        inverse = jnp.where(on_diagonal, 1.0 / jnp.where(on_diagonal, dm[i], 1.0), 0.0)
        gt[i, 0, pl.ds(their_rows, 64), :] += ct[i * SLOTS].astype(jnp.float32) - inverse * weight
        return carry

    lax.fori_loop(0, 4, settle, 0)
    settled = 4
    for leg in range(2):
        for u in range(2):
            for r in range(3):
                back(leg, r, u).wait_recv()
                back(leg + 1, r, u).start()
            lax.fori_loop(settled, settled + 3, settle, 0)
            settled += 3
    for u in range(2):
        for r in range(3):
            back(2, r, u).wait_recv()

    def result(i):
        return pltpu.make_async_copy(
            gt.at[i, :, pl.ds(their_rows, 64), :], out_ref.at[i], out_sem.at[i]
        )

    def pick(i, carry):
        for s in range(1, SLOTS):
            e = i * SLOTS + s
            low, high = [], []
            for r in range(3):
                c, b, a, k = split(idx_ref, r, e)
                for u, kept_rows in enumerate((low, high)):
                    kept_rows.append(fin2[c, b, a, 0, slice(*cut(r, u)[2:]), :])
            use_high = jnp.full((64, LANES), k, jnp.int32) > 0
            gt[i, s, pl.ds(their_rows, 64), :] += jnp.where(
                use_high,
                jnp.concatenate(high, axis=0).astype(jnp.float32),
                jnp.concatenate(low, axis=0).astype(jnp.float32),
            )
        result(i).start()
        return carry

    lax.fori_loop(0, ROWS, pick, 0)
    for ring in tables:
        ring.wait_send()
    for p in range(2, PARTS):
        first_sent(p)
    for p in range(PARTS):
        for r in range(3):
            third(p, r).wait_send()
    for leg in range(3):
        for r in range(3):
            for u in range(2):
                back(leg, r, u).wait_send()

    def drain(i, carry):
        to_sibling(i).wait_send()
        result(i).wait()
        return carry

    lax.fori_loop(0, ROWS, drain, 0)


def end_kernel(scale, h_ref, combined_ref, om_ref, grad_ref, next_ref):
    edge = STEP * PENALTY
    row = lax.broadcasted_iota(jnp.int32, (64, BW), 0) + h_ref[0] * 64
    diagonal = row == lax.broadcasted_iota(jnp.int32, (64, BW), 1)
    for i in range(END_ROWS):
        for s in range(SLOTS):
            grad = combined_ref[i, s] * scale
            trial = om_ref[i, s] - STEP * grad
            shrunk = jnp.where(
                trial > edge, trial - edge, jnp.where(trial < -edge, trial + edge, 0.0)
            )
            grad_ref[i, s] = grad
            next_ref[i, s] = jnp.where(diagonal, trial, shrunk) if s == 0 else shrunk


def index_tables(block_cols):
    entry = jnp.arange(ENTRIES, dtype=jnp.int32)
    cols = block_cols.reshape(ENTRIES)
    owner = cols // ROWS
    slot = entry % SLOTS
    remote = slot != 0
    named = (owner[None, :] == jnp.arange(64, dtype=jnp.int32)[:, None]) & remote[None, :]
    low = jnp.min(jnp.where(named, entry[None, :], ENTRIES - 1), axis=1)
    high = jnp.max(jnp.where(named, entry[None, :], 0), axis=1)
    table = jnp.pad(jnp.stack([low, high, low // SLOTS, high // SLOTS]), ((0, 4), (0, 64)))
    key = (cols % ROWS) * SLOTS + slot
    before = (owner[:, None] == owner[None, :]) & remote[None, :] & (key[None, :] < key[:, None])
    second = jnp.any(before, axis=1).astype(jnp.int32)
    return table, jnp.stack([owner // 16, (owner // 4) % 4, owner % 4, second])


def on_device(voxel_data, omega_blocks, block_cols):
    samples = voxel_data.shape[1] * lax.axis_size("samp")
    panels = voxel_data.reshape(ROWS, BW, voxel_data.shape[1])
    table, index = index_tables(block_cols)
    vmem, smem, hbm = pltpu.VMEM, pltpu.SMEM, pl.ANY
    bf16, f32, i32 = jnp.bfloat16, jnp.float32, jnp.int32
    dma = pltpu.SemaphoreType.DMA
    spec = pl.BlockSpec
    combined, _ = pl.pallas_call(
        functools.partial(step_kernel, 2.0 * samples),
        name="concord_exchange",
        out_shape=(
            jax.ShapeDtypeStruct((ROWS, SLOTS, 64, BW), f32),
            jax.ShapeDtypeStruct((PARTS, 4, 4, 4, 2, BW, LANES), bf16),
        ),
        in_specs=[
            spec(memory_space=hbm),
            spec(memory_space=hbm),
            spec(memory_space=vmem),
            spec(memory_space=smem),
        ],
        out_specs=(spec(memory_space=hbm),) * 2,
        scratch_shapes=[vmem((64, BW, LANES), bf16)] * PARTS
        + [vmem((4, 4, 4, 2, BW, LANES), bf16)] * PARTS
        + [
            vmem((3, 3, 4, 4, 2, BW, LANES), bf16),
            vmem((4, 4, 2, BW, LANES), bf16),
            vmem((ROWS, SLOTS, BW, BW), f32),
            vmem((2, SLOTS * BW, 3 * LANES), bf16),
            vmem((4, SLOTS, BW, BW), f32),
            vmem((SLOTS, BW, BW), f32),
            vmem((ENTRIES, 64, BW), bf16),
            vmem((ROWS, 64, BW), f32),
            vmem((3, 4, 8, 128), i32),
            smem((3, 4, 8, 128), i32),
            dma((3, 4)), dma((3, 4)), dma,
            dma((PARTS, 3, 4)), dma((PARTS, 3, 4)), dma((PARTS, 3)),
            dma((PARTS, 3, 4)), dma((PARTS, 3, 4)),
            dma((PARTS, 3, 4)), dma((PARTS, 3, 4)),
            dma((4,)), dma, dma((ROWS,)), dma((ROWS,)), dma((ROWS,)),
            dma((3, 6, 4)), dma((3, 6, 4)),
            pltpu.SemaphoreType.REGULAR,
        ],
        compiler_params=pltpu.CompilerParams(
            collective_id=0, has_side_effects=True, vmem_limit_bytes=63 << 20
        ),
    )(panels, omega_blocks, table, index)
    h = lax.axis_index("samp").astype(i32).reshape(1)
    tile = (END_ROWS, SLOTS, 64, BW)
    same = spec(tile, lambda i, h_ref: (i, 0, 0, 0))
    return pl.pallas_call(
        functools.partial(end_kernel, 0.5 / samples),
        name="proximal_end",
        out_shape=(jax.ShapeDtypeStruct((ROWS, SLOTS, 64, BW), f32),) * 2,
        grid_spec=pltpu.PrefetchScalarGridSpec(
            num_scalar_prefetch=1,
            grid=(ROWS // END_ROWS,),
            in_specs=[same, spec(tile, lambda i, h_ref: (i, 0, h_ref[0], 0))],
            out_specs=(same, same),
        ),
        compiler_params=pltpu.CompilerParams(vmem_limit_bytes=63 << 20),
    )(h, combined, omega_blocks)


def solution(mesh):
    in_specs = (P("vars", "samp"), P("vars", None, None, None), P("vars", None))
    out_specs = (P("vars", None, "samp", None), P("vars", None, "samp", None))
    return jax.shard_map(
        on_device, mesh=mesh, in_specs=in_specs, out_specs=out_specs, check_vma=False
    )
```

```python
import functools

import jax
import jax.numpy as jnp
from jax import lax
from jax.experimental import pallas as pl
from jax.experimental.pallas import tpu as pltpu
from jax.sharding import PartitionSpec as P

STEP = 0.5
PENALTY = 0.1
MESH = pl.DeviceIdType.MESH
RING = 4
STRIDES = (16, 4, 1)
BW = 128
ROWS = 16
SLOTS = 8
ENTRIES = ROWS * SLOTS
LANES = 128
PARTS = 6
PIECES = (((0, 32), (32, 80), (80, 128)), ((0, 48), (48, 80), (80, 128)), ((0, 48), (48, 96), (96, 128)))
GROUPS = ((0, 1, 2), (3, 4), (5,))
END_ROWS = 4
NEAR = (1, 3, 2)
CUTS = (((0, 16), (0, 16)), ((16, 32), (16, 48)), ((32, 64), (48, 64)))


def place():
    v = lax.axis_index("vars")
    at = (v // 16, lax.rem(v // 4, RING), lax.rem(v, RING))
    return v, at, lax.axis_index("samp")


def orders(r):
    return r % 3, (r + 1) % 3, (r + 2) % 3


def moved(v, at, axis, delta):
    there = lax.rem(at[axis] + delta, RING)
    return there, v + (there - at[axis]) * STRIDES[axis]


def greet(v, at, h, semaphore):
    for axis in range(3):
        for delta in NEAR:
            pl.semaphore_signal(
                semaphore, inc=1, device_id=(moved(v, at, axis, delta)[1], h), device_id_type=MESH
            )
    pl.semaphore_signal(semaphore, inc=1, device_id=(v, 1 - h), device_id_type=MESH)


def split(idx_ref, r, e):
    a, b, c = orders(r)
    return idx_ref[c, e], idx_ref[b, e], idx_ref[a, e], idx_ref[3, e]


class Ring:
    def __init__(self, v, at, h, axis, source, landing, send, recv):
        self.v, self.at, self.h, self.axis = v, at, h, axis
        self.source, self.landing, self.send, self.recv = source, landing, send, recv

    def remote(self, delta):
        there, target = moved(self.v, self.at, self.axis, delta)
        mine = self.at[self.axis]
        return pltpu.make_async_remote_copy(
            src_ref=self.source(there, delta),
            dst_ref=self.landing(mine),
            send_sem=self.send(delta),
            recv_sem=self.recv(mine),
            device_id=(target, self.h),
            device_id_type=MESH,
        )

    def arriving(self, delta):
        there, target = moved(self.v, self.at, self.axis, delta)
        return pltpu.make_async_remote_copy(
            src_ref=self.source(there, delta),
            dst_ref=self.landing(there),
            send_sem=self.send(delta),
            recv_sem=self.recv(there),
            device_id=(target, self.h),
            device_id_type=MESH,
        )

    def local(self):
        mine = self.at[self.axis]
        return pltpu.make_async_copy(self.source(mine, 0), self.landing(mine), self.recv(mine))

    def start(self):
        for delta in NEAR:
            self.remote(delta).start()
        self.local().start()

    def wait_recv(self):
        for delta in NEAR:
            self.arriving(delta).wait_recv()
        self.local().wait()

    def wait_send(self):
        for delta in NEAR:
            self.remote(delta).wait_send()


def step_kernel(
    weight,
    x_ref, om_ref, tab_ref, idx_ref,
    out_ref, s2_ref,
    ag0, ag1, ag2, ag3, ag4, ag5,
    fin0, fin1, fin2, fin3, fin4, fin5,
    st, sto, gt, xc, omv, rt, ct, dm, tabv, tabs,
    tab_s, tab_r, tab_c, s1s, s1r, s1l, s2s, s2r, s3s, s3r,
    om_sem, dm_sem, out_sem, sib_s, sib_r, back_s, back_r, free,
):
    v, at, h = place()
    ag = (ag0, ag1, ag2, ag3, ag4, ag5)
    fin = (fin0, fin1, fin2, fin3, fin4, fin5)
    greet(v, at, h, pltpu.get_barrier_semaphore())
    pl.semaphore_wait(pltpu.get_barrier_semaphore(), 10)

    tables = [
        Ring(
            v, at, h, axis,
            lambda there, delta: tab_ref,
            lambda mine, axis=axis: tabv.at[axis, mine],
            lambda delta, axis=axis: tab_s.at[axis, delta],
            lambda mine, axis=axis: tab_r.at[axis, mine],
        )
        for axis in range(3)
    ]

    def piece(p, r):
        low, high = PIECES[p % 3][r]
        return slice(low, high)

    def leg_of(p, r, delta, second_leg, arriving):
        axis = orders(r)[0]
        slot = (0 if delta == 1 else 1) + (2 if second_leg else 0)
        _, target = moved(v, at, axis, delta)
        back = RING - delta
        origin = lax.rem(at[axis] + back * (int(second_leg) + int(arriving)), RING)
        if second_leg:
            rows = pl.ds(origin * ROWS + (0 if delta == 1 else 8), 8)
        else:
            rows = pl.ds(origin * ROWS, ROWS)
        landing = ag[p].at[rows, piece(p, r)]
        if second_leg or arriving:
            source = landing
        else:
            source = x_ref.at[:, piece(p, r), pl.ds(p * LANES, LANES)]
        return pltpu.make_async_remote_copy(
            src_ref=source,
            dst_ref=landing,
            send_sem=s1s.at[p, r, slot],
            recv_sem=s1r.at[p, r, slot],
            device_id=(target, h),
            device_id_type=MESH,
        )

    def own_panels(p, r):
        return pltpu.make_async_copy(
            x_ref.at[:, piece(p, r), pl.ds(p * LANES, LANES)],
            ag[p].at[pl.ds(at[orders(r)[0]] * ROWS, ROWS), piece(p, r)],
            s1l.at[p, r],
        )

    def first_start(p):
        for r in range(3):
            leg_of(p, r, 1, False, False).start()
            leg_of(p, r, 3, False, False).start()
        for r in range(3):
            own_panels(p, r).start()

    def first_turn(p):
        for r in range(3):
            for delta in (1, 3):
                leg_of(p, r, delta, False, True).wait_recv()
                leg_of(p, r, delta, True, False).start()

    def first_sent(p):
        for r in range(3):
            for delta in (1, 3):
                for second_leg in (False, True):
                    leg_of(p, r, delta, second_leg, False).wait_send()

    def first_wait(p, r):
        for delta in (1, 3):
            leg_of(p, r, delta, True, True).wait_recv()
        own_panels(p, r).wait()

    def second(p, r):
        rows = piece(p, r)
        return Ring(
            v, at, h, orders(r)[1],
            lambda there, delta: (
                st.at[p % 3, delta - 1, :, :, :, rows] if delta else sto.at[:, :, :, rows]
            ),
            lambda mine: s2_ref.at[p, :, mine, :, :, rows],
            lambda delta: s2s.at[p, r, delta],
            lambda mine: s2r.at[p, r, mine],
        )

    def third(p, r):
        rows = piece(p, r)
        return Ring(
            v, at, h, orders(r)[2],
            lambda there, delta: s2_ref.at[p, there, :, :, :, rows],
            lambda mine: fin[p].at[mine, :, :, :, rows],
            lambda delta: s3s.at[p, r, delta],
            lambda mine: s3r.at[p, r, mine],
        )

    def stage(p, r):
        a_axis, b_axis, c_axis = orders(r)
        ring = second(p, r)
        rows = piece(p, r)
        for delta in (1, 3, 2, 0):
            there = lax.rem(at[b_axis] + delta, RING)
            base = at[a_axis] * STRIDES[a_axis] + there * STRIDES[b_axis]
            held = st.at[p % 3, delta - 1] if delta else sto

            def fill(c, carry):
                target = base + c * STRIDES[c_axis]
                for a in range(4):
                    for k in range(2):
                        row = a * ROWS + tabs[a_axis, a, 2 + k, target]
                        held[c, a, k, rows, :] = ag[p][row, rows, :]
                return carry

            lax.fori_loop(0, RING, fill, 0)
            if delta:
                ring.remote(delta).start()
            else:
                ring.local().start()

    def second_start(p):
        if p >= 3:
            for r in range(3):
                second(p - 3, r).wait_send()
        for r in range(3):
            first_wait(p, r)
        for r in range(3):
            stage(p, r)
        for r in range(3):
            second(p, r).local().wait()

    def third_start(p):
        for r in range(3):
            for delta in NEAR:
                second(p, r).arriving(delta).wait_recv()
            third(p, r).start()

    def third_wait(p):
        for r in range(3):
            third(p, r).wait_recv()

    def omega(i, slot):
        return pltpu.make_async_copy(om_ref.at[i], omv.at[slot], om_sem.at[slot])

    def to_sibling(i):
        return pltpu.make_async_remote_copy(
            src_ref=st.at[i // 12, lax.rem(i // 4, 3), lax.rem(i, 4)],
            dst_ref=fin0.at[i // 4, lax.rem(i, 4)],
            send_sem=sib_s.at[i],
            recv_sem=sib_r.at[i],
            device_id=(v, 1 - h),
            device_id_type=MESH,
        )

    mine_rows = pl.multiple_of(h * 64, 64)
    their_rows = pl.multiple_of((1 - h) * 64, 64)

    def kept(j, n):
        return ag[n].at[pl.ds(j * SLOTS, SLOTS)]

    def compute(group):
        if group < 2:
            for n in range(2):
                omega(n, n).start()

        width = len(GROUPS[group]) * LANES
        wide = 2 if group == len(GROUPS) - 1 else 1

        def pair(j, carry):
            held = []
            todo = [(m, n, (j * wide + m) * 2 + n) for m in range(wide) for n in range(2)]
            for m, n, i in todo:
                for q, p in enumerate(GROUPS[group]):
                    cols = slice((q + m) * LANES, (q + m + 1) * LANES)
                    for r in range(3):
                        rows = piece(p, r)
                        own = at[orders(r)[0]] * ROWS + i
                        xc[n, rows, cols] = ag[p][own, rows, :]
                    for s in range(1, SLOTS):
                        for r in range(3):
                            low, high = PIECES[p % 3][r]
                            c, b, a, k = split(idx_ref, r, i * SLOTS + s)
                            xc[n, s * BW + low : s * BW + high, cols] = fin[p][
                                c, b, a, k, low:high, :
                            ]
                if group < 2:
                    slot = lax.rem(j, 2) * 2 + n
                    omega(i, slot).wait()

                    @pl.when(j + 1 < ROWS // 2)
                    def _():
                        omega(i + 2, (1 - lax.rem(j, 2)) * 2 + n).start()

                    blocks = omv[slot].astype(jnp.bfloat16)
                    if group == 1:
                        kept(j, n)[...] = blocks
                else:
                    blocks = kept(j * wide + m, n)[...]
                held.append(jnp.concatenate([blocks[s] for s in range(SLOTS)], axis=1))
            w = [
                jnp.dot(
                    block, xc[n, :, m * LANES : m * LANES + width], preferred_element_type=jnp.float32
                ).astype(jnp.bfloat16)
                for block, (m, n, i) in zip(held, todo)
            ]
            for rows, (m, n, i) in zip(w, todo):
                turned = lax.dot_general(
                    xc[n, :, m * LANES : m * LANES + width], rows, (((1,), (1,)), ((), ())), preferred_element_type=jnp.float32
                ).reshape(SLOTS, BW, BW)
                if group == 0:
                    gt[i] = turned
                elif group < len(GROUPS) - 1:
                    gt[i] += turned
                else:
                    total = gt[i] + turned
                    gt[i] = total
                    theirs = st.at[i // 12, lax.rem(i // 4, 3), lax.rem(i, 4)]
                    theirs[...] = total.astype(jnp.bfloat16).reshape(4, 2, BW, BW)
                    to_sibling(i).start()
            return carry

        lax.fori_loop(0, ROWS // (2 * wide), pair, 0)

    diagonals = pltpu.make_async_copy(om_ref.at[:, 0, pl.ds(mine_rows, 64), :], dm, dm_sem)
    diagonals.start()
    first_start(0)
    for ring in tables:
        ring.start()
    first_start(1)
    first_turn(0)
    first_start(2)
    first_turn(1)
    for ring in tables:
        ring.wait_recv()
    copy = pltpu.make_async_copy(tabv, tabs, tab_c)
    copy.start()
    copy.wait()
    second_start(0)
    first_start(3)
    first_turn(2)
    second_start(1)
    first_start(4)
    first_turn(3)
    third_start(0)
    second_start(2)
    first_start(5)
    first_turn(4)
    third_start(1)
    second_start(3)
    first_turn(5)
    third_start(2)
    second_start(4)
    third_start(3)
    for p in range(3):
        third_wait(p)
    second_start(5)
    compute(0)
    greet(v, at, h, free)
    third_start(4)
    third_start(5)
    third_wait(3)
    third_wait(4)
    for p in range(2):
        first_sent(p)
    compute(1)
    for p in range(3, 6):
        for r in range(3):
            second(p, r).wait_send()
    pl.semaphore_wait(free, 10)
    third_wait(5)
    compute(2)

    def add(i, carry):
        to_sibling(i).wait_recv()
        mine = gt[i, :, pl.ds(mine_rows, 64), :]
        theirs = fin0[i // 4, lax.rem(i, 4), :, :, pl.ds(mine_rows, 64), :].reshape(SLOTS, 64, BW)
        ct[pl.ds(i * SLOTS, SLOTS)] = (mine + theirs.astype(jnp.float32)).astype(jnp.bfloat16)
        return carry

    lax.fori_loop(0, ROWS, add, 0, unroll=2)

    def cut(r, u):
        low, high = CUTS[r][u]
        start = sum(pair[0][1] - pair[0][0] + pair[1][1] - pair[1][0] for pair in CUTS[:r])
        start += (CUTS[r][0][1] - CUTS[r][0][0]) * u
        return low, high, start, start + high - low

    def back(leg, r, u):
        rows = slice(*cut(r, u)[2:])
        source = (
            lambda there, delta: fin2.at[there, :, :, 1, rows, :],
            lambda there, delta: fin1.at[there, :, :, 0, rows, :],
            lambda there, delta: fin1.at[there, :, :, 1, rows, :],
        )
        landing = (
            lambda mine: fin1.at[:, :, mine, 0, rows, :],
            lambda mine: fin1.at[:, mine, :, 1, rows, :],
            lambda mine: fin2.at[mine, :, :, 0, rows, :],
        )
        return Ring(
            v, at, h, orders(r)[leg], source[leg], landing[leg],
            lambda delta: back_s.at[leg, r * 2 + u, delta],
            lambda mine: back_r.at[leg, r * 2 + u, mine],
        )

    for u in range(2):
        for r in range(3):
            a_axis, b_axis, c_axis = orders(r)
            low, high, start, end = cut(r, u)

            def fill(n, carry):
                a, b = n // 4, lax.rem(n, 4)
                for c in range(4):
                    target = a * STRIDES[a_axis] + b * STRIDES[b_axis] + c * STRIDES[c_axis]
                    entry = tabs[0, at[0], u, target]
                    fin2[a, b, c, 1, start:end, :] = ct[entry, low:high, :]
                return carry

            lax.fori_loop(0, 16, fill, 0)
            back(0, r, u).start()

    on_diagonal = lax.broadcasted_iota(jnp.int32, (64, BW), 0) + mine_rows == (
        lax.broadcasted_iota(jnp.int32, (64, BW), 1)
    )
    diagonals.wait()

    def settle(i, carry):
        for s in range(SLOTS):
            theirs = fin0[i // 4, lax.rem(i, 4), s // 2, s % 2].astype(jnp.float32)
            rt[s] = (gt[i, s] + theirs).T
        gt[i, :, pl.ds(their_rows, 64), :] = rt[:, pl.ds(mine_rows, 64), :]
        inverse = jnp.where(on_diagonal, 1.0 / jnp.where(on_diagonal, dm[i], 1.0), 0.0)
        gt[i, 0, pl.ds(their_rows, 64), :] += ct[i * SLOTS].astype(jnp.float32) - inverse * weight
        return carry

    lax.fori_loop(0, 4, settle, 0)
    settled = 4
    for leg in range(2):
        for u in range(2):
            for r in range(3):
                back(leg, r, u).wait_recv()
                back(leg + 1, r, u).start()
            lax.fori_loop(settled, settled + 3, settle, 0)
            settled += 3
    for u in range(2):
        for r in range(3):
            back(2, r, u).wait_recv()

    def result(i):
        return pltpu.make_async_copy(
            gt.at[i, :, pl.ds(their_rows, 64), :], out_ref.at[i], out_sem.at[i]
        )

    def pick(i, carry):
        for s in range(1, SLOTS):
            e = i * SLOTS + s
            low, high = [], []
            for r in range(3):
                c, b, a, k = split(idx_ref, r, e)
                for u, kept_rows in enumerate((low, high)):
                    kept_rows.append(fin2[c, b, a, 0, slice(*cut(r, u)[2:]), :])
            use_high = jnp.full((64, LANES), k, jnp.int32) > 0
            gt[i, s, pl.ds(their_rows, 64), :] += jnp.where(
                use_high,
                jnp.concatenate(high, axis=0).astype(jnp.float32),
                jnp.concatenate(low, axis=0).astype(jnp.float32),
            )
        result(i).start()
        return carry

    lax.fori_loop(0, ROWS, pick, 0, unroll=2)
    for ring in tables:
        ring.wait_send()
    for p in range(2, PARTS):
        first_sent(p)
    for p in range(PARTS):
        for r in range(3):
            third(p, r).wait_send()
    for leg in range(3):
        for r in range(3):
            for u in range(2):
                back(leg, r, u).wait_send()

    def drain(i, carry):
        to_sibling(i).wait_send()
        result(i).wait()
        return carry

    lax.fori_loop(0, ROWS, drain, 0)


def end_kernel(scale, h_ref, combined_ref, om_ref, grad_ref, next_ref):
    edge = STEP * PENALTY
    row = lax.broadcasted_iota(jnp.int32, (64, BW), 0) + h_ref[0] * 64
    diagonal = row == lax.broadcasted_iota(jnp.int32, (64, BW), 1)
    for i in range(END_ROWS):
        for s in range(SLOTS):
            grad = combined_ref[i, s] * scale
            trial = om_ref[i, s] - STEP * grad
            shrunk = jnp.where(
                trial > edge, trial - edge, jnp.where(trial < -edge, trial + edge, 0.0)
            )
            grad_ref[i, s] = grad
            next_ref[i, s] = jnp.where(diagonal, trial, shrunk) if s == 0 else shrunk


def index_tables(block_cols):
    entry = jnp.arange(ENTRIES, dtype=jnp.int32)
    cols = block_cols.reshape(ENTRIES)
    owner = cols // ROWS
    slot = entry % SLOTS
    remote = slot != 0
    named = (owner[None, :] == jnp.arange(64, dtype=jnp.int32)[:, None]) & remote[None, :]
    low = jnp.min(jnp.where(named, entry[None, :], ENTRIES - 1), axis=1)
    high = jnp.max(jnp.where(named, entry[None, :], 0), axis=1)
    table = jnp.pad(jnp.stack([low, high, low // SLOTS, high // SLOTS]), ((0, 4), (0, 64)))
    key = (cols % ROWS) * SLOTS + slot
    before = (owner[:, None] == owner[None, :]) & remote[None, :] & (key[None, :] < key[:, None])
    second = jnp.any(before, axis=1).astype(jnp.int32)
    return table, jnp.stack([owner // 16, (owner // 4) % 4, owner % 4, second])


def on_device(voxel_data, omega_blocks, block_cols):
    samples = voxel_data.shape[1] * lax.axis_size("samp")
    panels = voxel_data.reshape(ROWS, BW, voxel_data.shape[1])
    table, index = index_tables(block_cols)
    vmem, smem, hbm = pltpu.VMEM, pltpu.SMEM, pl.ANY
    bf16, f32, i32 = jnp.bfloat16, jnp.float32, jnp.int32
    dma = pltpu.SemaphoreType.DMA
    spec = pl.BlockSpec
    combined, _ = pl.pallas_call(
        functools.partial(step_kernel, 2.0 * samples),
        name="concord_exchange",
        out_shape=(
            jax.ShapeDtypeStruct((ROWS, SLOTS, 64, BW), f32),
            jax.ShapeDtypeStruct((PARTS, 4, 4, 4, 2, BW, LANES), bf16),
        ),
        in_specs=[
            spec(memory_space=hbm),
            spec(memory_space=hbm),
            spec(memory_space=vmem),
            spec(memory_space=smem),
        ],
        out_specs=(spec(memory_space=hbm),) * 2,
        scratch_shapes=[vmem((64, BW, LANES), bf16)] * PARTS
        + [vmem((4, 4, 4, 2, BW, LANES), bf16)] * PARTS
        + [
            vmem((3, 3, 4, 4, 2, BW, LANES), bf16),
            vmem((4, 4, 2, BW, LANES), bf16),
            vmem((ROWS, SLOTS, BW, BW), f32),
            vmem((2, SLOTS * BW, 3 * LANES), bf16),
            vmem((4, SLOTS, BW, BW), f32),
            vmem((SLOTS, BW, BW), f32),
            vmem((ENTRIES, 64, BW), bf16),
            vmem((ROWS, 64, BW), f32),
            vmem((3, 4, 8, 128), i32),
            smem((3, 4, 8, 128), i32),
            dma((3, 4)), dma((3, 4)), dma,
            dma((PARTS, 3, 4)), dma((PARTS, 3, 4)), dma((PARTS, 3)),
            dma((PARTS, 3, 4)), dma((PARTS, 3, 4)),
            dma((PARTS, 3, 4)), dma((PARTS, 3, 4)),
            dma((4,)), dma, dma((ROWS,)), dma((ROWS,)), dma((ROWS,)),
            dma((3, 6, 4)), dma((3, 6, 4)),
            pltpu.SemaphoreType.REGULAR,
        ],
        compiler_params=pltpu.CompilerParams(
            collective_id=0, has_side_effects=True, vmem_limit_bytes=63 << 20
        ),
    )(panels, omega_blocks, table, index)
    h = lax.axis_index("samp").astype(i32).reshape(1)
    tile = (END_ROWS, SLOTS, 64, BW)
    same = spec(tile, lambda i, h_ref: (i, 0, 0, 0))
    return pl.pallas_call(
        functools.partial(end_kernel, 0.5 / samples),
        name="proximal_end",
        out_shape=(jax.ShapeDtypeStruct((ROWS, SLOTS, 64, BW), f32),) * 2,
        grid_spec=pltpu.PrefetchScalarGridSpec(
            num_scalar_prefetch=1,
            grid=(ROWS // END_ROWS,),
            in_specs=[same, spec(tile, lambda i, h_ref: (i, 0, h_ref[0], 0))],
            out_specs=(same, same),
        ),
        compiler_params=pltpu.CompilerParams(vmem_limit_bytes=63 << 20),
    )(h, combined, omega_blocks)


def solution(mesh):
    in_specs = (P("vars", "samp"), P("vars", None, None, None), P("vars", None))
    out_specs = (P("vars", None, "samp", None), P("vars", None, "samp", None))
    return jax.shard_map(
        on_device, mesh=mesh, in_specs=in_specs, out_specs=out_specs, check_vma=False
    )
```
